32 devices in a mesh: pts: 16 (over z, x, core), dom: 2 (over y).
Axes of the slice: x: 2, y: 2, z: 4, core: 2. Of those that a mesh axis runs over, the one named last changes fastest.
Arguments:
- vectors: bfloat16 [2, 4096, 768], P('dom', 'pts'), may hold values from -6 to 6
- neighbor_shards: int32 [2, 4096, 1], P('dom', 'pts'), may hold values from 0 to 15, as said below
- neighbor_locals: int32 [2, 4096, 32], P('dom', 'pts'), may hold values from 0 to 255
- partition: int32 [2, 4096], P('dom', 'pts'), may hold values from 0 to 1, as said below
Outputs:
- moved_vectors: bfloat16 [2, 4096, 768], P('dom', 'pts')
- moved_reverse: bfloat16 [2, 4096, 32], P('dom', 'pts')
- moved_join: bfloat16 [2, 4096, 32], P('dom', 'pts')
The draws below stay inside these ranges and needn't reach their ends.
Inputs may be any that keep to these rules, and one draw needn't show every extreme that they name: `neighbor_shards`: the 1 numbers of one row are distinct, and the rows of one device come in aligned runs of 8 rows with equal numbers. Among the 256 rows of one device no number appears in more than 32 rows, and one number appears in exactly 32 rows. `partition`: for each id range, the 512 points of that range over all domains are split into 2 partitions of exactly 256 points each.
All inputs are finite; a program needn't handle non-finite values.
Results may differ from the reference program's by a relative error of at most 0.001.
Values may be sent and summed in bfloat16 or wider, within the bound.
A program may use at most 64 MiB of HBM per device.

```python
import jax
import jax.numpy as jnp
import numpy as np
from jax import lax

D = 768
K = 32
R = 32
P_DEV = 256
W = 1
CAP = 32
GRP = 8
DOMS = 2
NP = 4096
N_PTS = 16


def draw_partition(key, part):
    base_key = jax.random.fold_in(key, 11)
    key_stay, key_other, key_jitter = jax.random.split(base_key, 3)
    grid_shape = (DOMS, N_PTS, P_DEV)
    stay_flag = jax.random.randint(key_stay, grid_shape, 0, 2)
    other_dom = jax.random.randint(key_other, grid_shape, 0, DOMS)
    dom_index = jnp.arange(DOMS, dtype=jnp.int32)[:, None, None]
    preferred = jnp.where(stay_flag == 1, dom_index, other_dom)
    jitter = jax.random.randint(key_jitter, grid_shape, 0, 4096)
    local_ids = dom_index * P_DEV + jnp.arange(P_DEV, dtype=jnp.int32)[None, None, :]
    scores = (preferred * 4096 + jitter) * (DOMS * P_DEV) + local_ids
    columns = jnp.transpose(scores, (1, 0, 2)).reshape(N_PTS, DOMS * P_DEV)
    ranking = jnp.argsort(jnp.argsort(columns, axis=1), axis=1)
    parts = (ranking // P_DEV).reshape(N_PTS, DOMS, P_DEV)
    return jnp.transpose(parts, (1, 0, 2)).reshape(DOMS, N_PTS * P_DEV).astype(jnp.int32)


def draw_neighbor_shards(key, part):
    base_key = jax.random.fold_in(key, 23)
    key_raw, key_bias, key_fixed, key_cells = jax.random.split(base_key, 4)
    layer_count = CAP // GRP
    half_count = N_PTS // 2
    target_ids = jnp.arange(N_PTS, dtype=jnp.int32)
    raw_scores = jax.random.randint(key_raw, (DOMS, N_PTS, layer_count, N_PTS), 0, 1 << 20)
    bias_level = jax.random.randint(key_bias, (DOMS, 1, 1, N_PTS), 0, 4) * (1 << 18)
    scores = (raw_scores + bias_level) * N_PTS + target_ids[None, None, None, :]
    fixed_target = jax.random.randint(key_fixed, (DOMS, N_PTS, 1, 1), 0, N_PTS)
    scores = jnp.where(target_ids[None, None, None, :] == fixed_target, -1, scores)
    chosen = jnp.argsort(scores, axis=-1)[..., :half_count].astype(jnp.int32)
    cell_count = layer_count * half_count // W
    cells = chosen.reshape(DOMS, N_PTS, cell_count, W)
    cell_scores = jax.random.randint(key_cells, (DOMS, N_PTS, cell_count), 0, 1 << 20) * cell_count + jnp.arange(cell_count, dtype=jnp.int32)[None, None, :]
    cell_order = jnp.argsort(cell_scores, axis=-1).astype(jnp.int32)
    cells = jnp.take_along_axis(cells, cell_order[..., None], axis=2)
    rows = jnp.repeat(cells, GRP, axis=2)
    return rows.reshape(DOMS, NP, W).astype(jnp.int32)


def draw_vectors(key, part):
    base_key = jax.random.fold_in(key, 31)
    key_signs, key_noise = jax.random.split(base_key)
    signs = (2 * jax.random.randint(key_signs, (DOMS, 1, D), 0, 2) - 1).astype(jnp.float32)
    local_ids = jnp.arange(NP, dtype=jnp.int32) % P_DEV
    close_rows = local_ids % (4 * GRP) == 0
    along = jnp.where(close_rows, 0.75, 0.35).astype(jnp.float32)[None, :, None]
    across = jnp.sqrt(1.0 - along * along)
    noise = jax.random.truncated_normal(key_noise, -4.0, 4.0, (DOMS, NP, D), jnp.float32)
    return (along * signs + across * noise).astype(jnp.bfloat16)


def plant(array, rng, least, largest):
    longest = array.shape.index(max(array.shape))
    spots = []
    for shift in (0, 1):
        where = [jax.random.randint(jax.random.fold_in(rng, axis), (), 0, length) for axis, length in enumerate(array.shape)]
        where[longest] = (where[longest] + shift) % array.shape[longest]
        spots.append(tuple(where))
    return array.at[spots[0]].set(least).at[spots[1]].set(largest)


def setup_inputs(seed: int = 0) -> dict:
    keys = jax.random.split(jax.random.key(seed), 5)
    return {
        "vectors": draw_vectors(jax.random.fold_in(keys[4], 71), 0),
        "neighbor_shards": draw_neighbor_shards(jax.random.fold_in(keys[4], 71), 0),
        "neighbor_locals": plant(jax.random.randint(keys[2], (DOMS, NP, K), 0, P_DEV), jax.random.fold_in(keys[2], 1), 0, P_DEV - 1).astype(jnp.int32),
        "partition": draw_partition(jax.random.fold_in(keys[4], 71), 0),
    }


BIG_VALUE = 1.0e9


def smallest_rows(distance, allowed):
    masked = jnp.where(allowed, distance, BIG_VALUE)
    lowest = -lax.top_k(-masked, R)[0]
    return jnp.where(lowest < 0.5 * BIG_VALUE, lowest, 0.0)


def regroup(values, order_cols):
    feature = values.shape[-1]
    columns = values.reshape(DOMS, N_PTS, P_DEV, feature).transpose(1, 0, 2, 3).reshape(N_PTS, DOMS * P_DEV, feature)
    taken = jnp.take_along_axis(columns, order_cols[:, :, None], axis=1)
    return taken.reshape(N_PTS, DOMS, P_DEV, feature).transpose(1, 0, 2, 3).reshape(DOMS, N_PTS * P_DEV, feature)


def reference(vectors, neighbor_shards, neighbor_locals, partition):
    cap_rows = N_PTS * CAP
    sq_norms = jnp.sum(jnp.square(vectors.astype(jnp.float32)), axis=-1)
    per_slot = neighbor_shards[:, :, np.arange(K) % W]
    global_nbr = (per_slot * P_DEV + neighbor_locals).astype(jnp.int32)

    def one_shard(shard_num):
        domain = shard_num // N_PTS
        column = shard_num % N_PTS
        dom_vec = lax.dynamic_index_in_dim(vectors, domain, 0, keepdims=False)
        dom_norm = lax.dynamic_index_in_dim(sq_norms, domain, 0, keepdims=False)
        dom_shards = lax.dynamic_index_in_dim(neighbor_shards, domain, 0, keepdims=False)
        dom_nbr = lax.dynamic_index_in_dim(global_nbr, domain, 0, keepdims=False)
        member = jnp.any(dom_shards == column, axis=1)
        picked = jnp.argsort(1 - member.astype(jnp.int32), stable=True)[:cap_rows].astype(jnp.int32)
        is_valid = member[picked]
        row_start = (column * P_DEV).astype(jnp.int32)
        own_vec = lax.dynamic_slice_in_dim(dom_vec, row_start, P_DEV, 0)
        own_norm = lax.dynamic_slice_in_dim(dom_norm, row_start, P_DEV, 0)
        inner_prod = jnp.dot(own_vec, dom_vec[picked].T, preferred_element_type=jnp.float32)
        distance = (own_norm[:, None] + dom_norm[picked][None, :] - 2.0 * inner_prod) / D
        own_ids = row_start + jnp.arange(P_DEV, dtype=jnp.int32)
        join_ok = is_valid[None, :] & (picked[None, :] != own_ids[:, None])
        listed = jnp.any(dom_nbr[picked][None, :, :] == own_ids[:, None, None], axis=-1)
        return smallest_rows(distance, join_ok & listed), smallest_rows(distance, join_ok)

    reverse_rows, join_rows = lax.map(one_shard, jnp.arange(DOMS * N_PTS, dtype=jnp.int32))
    reverse_rows = reverse_rows.reshape(DOMS, NP, R).astype(jnp.bfloat16)
    join_rows = join_rows.reshape(DOMS, NP, R).astype(jnp.bfloat16)
    part_cols = partition.reshape(DOMS, N_PTS, P_DEV).transpose(1, 0, 2).reshape(N_PTS, DOMS * P_DEV)
    order_cols = jnp.argsort(part_cols, axis=1, stable=True).astype(jnp.int32)
    return (regroup(vectors, order_cols), regroup(reverse_rows, order_cols), regroup(join_rows, order_cols))
```

```python
import functools

import jax
import jax.numpy as jnp
from jax import lax
from jax.experimental import pallas as pl
from jax.experimental.pallas import tpu as pltpu
from jax.sharding import PartitionSpec as P

R = 32
BIG = 1.0e9
NT = (((1,), (1,)), ((), ()))

START = (0, 1, 2, 4, 3)
SORT = (
    ((0,),),
    ((1,), (1, 2), (0,)),
    ((1,), (1, 2), (1,), (0,)),
    ((0, 4), (0,), (0, 2), (0,), (1,), (1, 4), (1,)),
    ((1, 3), (1,), (1, 2), (1,), (0,), (0, 4), (0,), (0, 3), (0,)),
)
MERGE = ((0, 3), (0, 2), (0,), (0, 2), (0, 4), (1,), (0,), (0, 4), (0,), (0, 3), (0,))
FINISH = ((0, 2),)


BATCHES = (4, 4, 4, 4)
ORDER = (8, 1, 9, 2, 10, 3, 11, 4, 12, 5, 13, 6, 14, 7, 15)
WAIT = (1, 2, 3, 8, 4, 9, 5, 10, 6, 11, 7, 12, 13, 14, 15)


def dot(a, b):
    return jnp.dot(a, b, preferred_element_type=jnp.float32)


def dot_nt(a, b):
    return lax.dot_general(a, b, NT, preferred_element_type=jnp.float32)


def iota(shape, dim):
    return lax.broadcasted_iota(jnp.int32, shape, dim)


def onehot(cond):
    return jnp.where(cond, 1.0, 0.0).astype(jnp.bfloat16)


def pairs_along(bit):
    return [(i, i | 1 << bit) for i in range(4) if not i >> bit & 1]


def run_steps(items, steps, falling=False):
    items = list(items)
    place = iota(items[0].shape, 0)
    for step in steps:
        for i, j in pairs_along(step[0]):
            a, b = items[i], items[j]
            if len(step) == 1:
                low, high = jnp.minimum(a, b), jnp.maximum(a, b)
                items[i], items[j] = (high, low) if falling else (low, high)
            else:
                far = 1 << step[1] - 2
                first = (place & far) == 0
                items[i] = jnp.where(first, a, pltpu.roll(b, far, 0))
                items[j] = jnp.where(first, pltpu.roll(a, 8 - far, 0), b)
    return items


def flip(items, bits):
    place = iota(items[0].shape, 0)
    rows = [b - 2 for b in bits if b > 1]
    out = []
    for i, x in enumerate(items):
        odd = sum(i >> b & 1 for b in bits if b < 2) & 1
        if rows:
            total = sum((place >> s) & 1 for s in rows)
            sign = jnp.where((total & 1) == odd, 1.0, -1.0)
            x = x * sign
        elif odd:
            x = -x
        out.append(x)
    return out


def sort_falling(items):
    where = list(START)
    negated = None
    for phase, steps in enumerate(SORT):
        bit = phase + 1
        bits = []
        if negated is not None:
            bits.append(where.index(negated))
        negated = bit if bit < 5 else None
        if negated is not None:
            bits.append(where.index(negated))
        items = flip(items, bits)
        items = run_steps(items, steps, falling=bit == 5)
        for step in steps:
            if len(step) == 2:
                v, s = step
                where[v], where[s] = where[s], where[v]
    return items


def merge_low(rising, falling):
    return run_steps([jnp.minimum(a, b) for a, b in zip(rising, falling)], MERGE)


def kernel(n, doms, cap, order, *refs):
    refs = list(refs)
    vec, shards_hbm, locs_hbm, part_hbm = refs[:4]
    refs = refs[4:]
    wide = shards_hbm.shape[0] > 1
    slot_shard_hbm = refs.pop(0) if wide else None
    out_vec, out_rows = refs[:2]
    (own_ref, shards_t, locs, part, slot_shard, sbuf, sinfo, rvec, rinfo, dvec, dpart, posn, ltile, lshard, selfid,
     onorm, best, picks, srows, drows,
     in_sem, vs_sem, vr_sem, is_sem, ir_sem, ds_sem, dr_sem, ps_sem, pr_sem, rs_sem, rr_sem) = refs[2:]
    per, depth = vec.shape
    list_len = locs.shape[0]
    groups = cap // 8
    lanes = groups * list_len
    me = lax.axis_index("pts")
    dom = lax.axis_index("dom")
    bar = pltpu.get_barrier_semaphore()
    bits = [1 << b for b in range(n.bit_length() - 1)]

    def partner(o):
        return me + sum(lax.rem(o // b, 2) * (b - 2 * b * lax.rem(me // b, 2)) for b in bits)

    def greet_pts(o, carry):
        pl.semaphore_signal(bar, inc=1, device_id={"pts": lax.rem(me + o, n)}, device_id_type=pl.DeviceIdType.MESH)
        return carry

    def greet_dom(o, carry):
        pl.semaphore_signal(bar, inc=1, device_id={"dom": lax.rem(dom + o, doms)}, device_id_type=pl.DeviceIdType.MESH)
        return carry

    fetch_shards = pltpu.make_async_copy(shards_hbm, shards_t, in_sem.at[0])
    fetch_locs = pltpu.make_async_copy(locs_hbm, locs, in_sem.at[1])
    fetch_part = pltpu.make_async_copy(part_hbm, part, in_sem.at[2])
    fetch_vec = pltpu.make_async_copy(vec, own_ref, in_sem.at[3])
    fetch_shards.start()
    fetch_vec.start()
    fetch_locs.start()
    if wide:
        fetch_slots = pltpu.make_async_copy(slot_shard_hbm, slot_shard, in_sem.at[4])
        fetch_slots.start()
    fetch_part.start()
    lax.fori_loop(1, n, greet_pts, 0)
    lax.fori_loop(1, doms, greet_dom, 0)

    upper = onehot(iota((per, per), 0) < iota((per, per), 1))
    tile = onehot(lax.rem(iota((list_len, lanes), 1), list_len) == iota((list_len, lanes), 0))
    targets = partner(iota((n, per), 0))
    lane_group = iota((8, lanes), 1) // list_len
    slot_row = iota((cap, per), 0).astype(jnp.float32)

    fetch_shards.wait()
    member = shards_t[0:1, :] == targets
    for w in range(1, shards_t.shape[0]):
        member = member | (shards_t[w : w + 1, :] == targets)
    rank = dot(onehot(member), upper)
    posn[...] = jnp.where(member, rank, -1.0)

    def spread(ref):
        return lax.dot_general(ref[...].astype(jnp.float32).astype(jnp.bfloat16), tile, (((0,), (0,)), ((), ())),
                               preferred_element_type=jnp.float32)

    fetch_locs.wait()
    ltile[...] = (spread(locs) + 1.0).astype(jnp.bfloat16)
    if wide:
        fetch_slots.wait()
        lshard[...] = spread(slot_shard)
    fetch_vec.wait()

    def fold(full):
        flat = jnp.zeros((8, lanes), jnp.float32)
        for g in range(groups):
            flat = jnp.where(lane_group == g, full[8 * g : 8 * g + 8], flat)
        return flat.astype(jnp.bfloat16)

    def pack(slots, offsets):
        picks_ = [onehot(posn[pl.ds(o, 1), :] == slot_row) for o in offsets]
        pick = jnp.concatenate(picks_, axis=0)
        if not wide:
            full = dot(pick, ltile[...])
        packed = dot(pick, own_ref[...]).astype(jnp.bfloat16)
        for t, (i, o) in enumerate(zip(slots, offsets)):
            if wide:
                c = partner(o)
                entry = jnp.where(lshard[...] == c.astype(jnp.float32), ltile[...].astype(jnp.float32), 0.0)
                sinfo[i] = fold(dot(picks_[t], entry.astype(jnp.bfloat16)))
            else:
                sinfo[i] = fold(full[t * cap : t * cap + cap])
            sbuf[i] = packed[t * cap : t * cap + cap]

    def vec_copy(i, c):
        return pltpu.make_async_remote_copy(
            src_ref=sbuf.at[i], dst_ref=rvec.at[i], send_sem=vs_sem.at[i], recv_sem=vr_sem.at[i],
            device_id={"pts": c}, device_id_type=pl.DeviceIdType.MESH)

    def info_copy(i, c):
        return pltpu.make_async_remote_copy(
            src_ref=sinfo.at[i], dst_ref=rinfo.at[i], send_sem=is_sem.at[i], recv_sem=ir_sem.at[i],
            device_id={"pts": c}, device_id_type=pl.DeviceIdType.MESH)

    def dom_copy(c, slot_r, src, dst, send, recv):
        return pltpu.make_async_remote_copy(
            src_ref=src, dst_ref=dst.at[slot_r], send_sem=send.at[c], recv_sem=recv.at[slot_r],
            device_id={"dom": c}, device_id_type=pl.DeviceIdType.MESH)

    def send(i, o):
        c = partner(o)
        info_copy(i, c).start()
        vec_copy(i, c).start()

    def send_dom(o, carry):
        c = lax.rem(dom + o, doms)
        dom_copy(c, dom, part, dpart, ps_sem, pr_sem).start()
        dom_copy(c, dom, own_ref, dvec, ds_sem, dr_sem).start()
        return carry

    def arrived():
        fetch_part.wait()
        pl.semaphore_wait(bar, n - 1 + doms - 1)
        lax.fori_loop(1, doms, send_dom, 0)

    if order is not None:
        whole = [(1 + WAIT.index(o), o) for o in order] + [(0, 0)]
        at = 0
        for size in BATCHES:
            some = whole[at : at + size]
            at += size
            pack([i for i, _ in some], [o for _, o in some])
            if at == size:
                arrived()
            for i, o in some:
                if o:
                    send(i, o)
    else:
        def pack_loop(b, carry):
            some = [b * 4 + t for t in range(4)]
            pack(some, some)
            return carry

        def send_loop(o, carry):
            send(o, o)
            return carry

        lax.fori_loop(0, n // 4, pack_loop, 0)
        arrived()
        lax.fori_loop(1, n, send_loop, 0)
    own = own_ref[...]
    square = jnp.square(own.astype(jnp.float32))
    high = square.astype(jnp.bfloat16)
    low = (square - high.astype(jnp.float32)).astype(jnp.bfloat16)
    ones = jnp.ones((8, depth), jnp.bfloat16)
    onorm[...] = dot_nt(ones, high) + dot_nt(ones, low)
    id_tile = (iota((per, 128), 0) + 1).astype(jnp.float32).astype(jnp.bfloat16)
    selfid[...] = dot(onehot(posn[0:1, :] == slot_row), id_tile)
    dvec[dom] = own
    dpart[dom] = part[...]
    width = shards_t.shape[0]
    for which in range(2):
        for v in range(4):
            best[which, v] = jnp.full((8, per), BIG, jnp.float32)

    def join(vectors, info, same):
        cand = vectors[...]
        wide_cand = cand.astype(jnp.float32)
        norm = jnp.sum(wide_cand * wide_cand, axis=1, keepdims=True)
        value = (onorm[0:1, :] + norm - 2.0 * dot_nt(cand, own_ref[...])) * (1.0 / depth)
        entry = info[...].astype(jnp.float32)
        point = (iota((8, per), 1) + 1).astype(jnp.float32)
        reverse, joined = [], []
        for g in range(groups):
            at = g * list_len
            listed = entry[:, at : at + 1] == point
            for k in range(1, list_len):
                listed = listed | (entry[:, at + k : at + k + 1] == point)
            allowed = entry[:, at : at + 1] > 0.0
            for w in range(1, width):
                allowed = allowed | (entry[:, at + w : at + w + 1] > 0.0)
            if same:
                allowed = allowed & (selfid[8 * g : 8 * g + 8, 0:1] != point)
            block = jnp.where(allowed, value[8 * g : 8 * g + 8], BIG)
            joined.append(block)
            reverse.append(jnp.where(listed, block, BIG))
        return reverse, joined

    def add(which, block):
        items = merge_low([best[which, v] for v in range(4)], sort_falling(block))
        for v in range(4):
            best[which, v] = items[v]

    def add_both(vectors, info, same):
        blocks = join(vectors, info, same)
        for which in range(2):
            add(which, blocks[which])

    add_both(sbuf.at[0], sinfo.at[0], True)
    other = lax.rem(me + 1, n)

    def take(i, carry):
        info_copy(i, other).wait_recv()
        vec_copy(i, other).wait_recv()
        add_both(rvec.at[i], rinfo.at[i], False)
        return carry

    def take_dom(o, carry):
        s = lax.rem(dom + doms - o, doms)
        dom_copy(s, s, part, dpart, ps_sem, pr_sem).wait_recv()
        dom_copy(s, s, own_ref, dvec, ds_sem, dr_sem).wait_recv()
        return carry

    lax.fori_loop(1, n // 2, take, 0)
    lax.fori_loop(1, doms, take_dom, 0)
    base = jnp.zeros((8, 1), jnp.float32)
    total = jnp.zeros((per, depth), jnp.float32)
    for d in range(doms):
        here = jnp.broadcast_to(dpart[d], (8, per)) == dom
        flag = jnp.where(here, 1.0, 0.0)
        place = jnp.where(here, dot(flag.astype(jnp.bfloat16), upper) + base, -1.0)
        base = base + jnp.sum(flag, axis=1, keepdims=True)
        pick = onehot(place[0:1, :] == iota((per, per), 0).astype(jnp.float32))
        picks[d] = pick
        total = total + dot(pick, dvec[d])
    out_vec[...] = total.astype(jnp.bfloat16)
    lax.fori_loop(n // 2, n, take, 0)

    def rows_copy(c, slot_r, which):
        return pltpu.make_async_remote_copy(
            src_ref=srows.at[which], dst_ref=drows.at[slot_r, which], send_sem=rs_sem.at[which, c],
            recv_sem=rr_sem.at[which, slot_r], device_id={"dom": c}, device_id_type=pl.DeviceIdType.MESH)

    for which in range(2):
        items = run_steps([best[which, v] for v in range(4)], FINISH)
        items = [items[v >> 1 | (v & 1) << 1] for v in range(4)]
        rows = jnp.concatenate([jnp.where(x < 0.5 * BIG, x, 0.0) for x in items], axis=0)
        srows[which] = rows.astype(jnp.bfloat16)

        def send_rows(o, carry):
            rows_copy(lax.rem(dom + o, doms), dom, which).start()
            return carry

        lax.fori_loop(1, doms, send_rows, 0)

    def drain_pts(i, carry):
        info_copy(i, other).wait_send()
        vec_copy(i, other).wait_send()
        return carry

    def drain_dom(o, carry):
        c = lax.rem(dom + o, doms)
        dom_copy(c, dom, part, dpart, ps_sem, pr_sem).wait_send()
        dom_copy(c, dom, own_ref, dvec, ds_sem, dr_sem).wait_send()
        return carry

    lax.fori_loop(1, n, drain_pts, 0)
    lax.fori_loop(1, doms, drain_dom, 0)
    moved = dot_nt(jnp.concatenate([srows[0], srows[1]], axis=0), picks[dom])
    for o in range(1, doms):
        s = lax.rem(dom + doms - o, doms)
        rows_copy(s, s, 0).wait_recv()
        rows_copy(s, s, 1).wait_recv()
        moved = moved + dot_nt(jnp.concatenate([drows[s, 0], drows[s, 1]], axis=0), picks[s])
    out_rows[...] = moved.astype(jnp.bfloat16)
    for o in range(1, doms):
        c = lax.rem(dom + o, doms)
        rows_copy(c, dom, 0).wait_send()
        rows_copy(c, dom, 1).wait_send()


def place(found_vec, found_rows, out_vec, out_rev, out_join):
    out_vec[...] = found_vec[...]
    out_rev[...] = found_rows[:R]
    out_join[...] = found_rows[R:]


def solution(mesh):
    n, doms = mesh.shape["pts"], mesh.shape["dom"]
    order = ORDER if n == 16 else None

    def per_device(vectors, neighbor_shards, neighbor_locals, partition):
        per, depth = vectors.shape[1:]
        width = neighbor_shards.shape[2]
        list_len = neighbor_locals.shape[2]
        cap = per // 8
        lanes = (cap // 8) * list_len
        assert cap == R
        operands = [vectors[0], neighbor_shards[0].T, neighbor_locals[0].T, partition]
        if width > 1:
            operands.append(neighbor_shards[0].T[jnp.arange(list_len) % width])
        bf16, f32, i32 = jnp.bfloat16, jnp.float32, jnp.int32
        dma = pltpu.SemaphoreType.DMA
        vmem = pl.BlockSpec(memory_space=pltpu.VMEM)
        anywhere = pl.BlockSpec(memory_space=pltpu.HBM)
        shapes = (jax.ShapeDtypeStruct((per, depth), bf16), jax.ShapeDtypeStruct((2 * R, per), bf16))
        found_vec, found_rows = pl.pallas_call(
            functools.partial(kernel, n, doms, cap, order),
            out_shape=shapes,
            in_specs=[anywhere] * len(operands),
            out_specs=(vmem, vmem),
            scratch_shapes=[
                pltpu.VMEM((per, depth), bf16),
                pltpu.VMEM((width, per), i32),
                pltpu.VMEM((list_len, per), i32),
                pltpu.VMEM((1, per), i32),
                pltpu.VMEM((list_len, per), i32),
                pltpu.VMEM((n, cap, depth), bf16),
                pltpu.VMEM((n, 8, lanes), bf16),
                pltpu.VMEM((n, cap, depth), bf16),
                pltpu.VMEM((n, 8, lanes), bf16),
                pltpu.VMEM((doms, per, depth), bf16),
                pltpu.VMEM((doms, 1, per), i32),
                pltpu.VMEM((n, per), f32),
                pltpu.VMEM((per, lanes), bf16),
                pltpu.VMEM((per, lanes), f32),
                pltpu.VMEM((cap, 128), f32),
                pltpu.VMEM((8, per), f32),
                pltpu.VMEM((2, 4, 8, per), f32),
                pltpu.VMEM((doms, per, per), bf16),
                pltpu.VMEM((2, R, per), bf16),
                pltpu.VMEM((doms, 2, R, per), bf16),
                dma((5,)),
                dma((n,)), dma((n,)), dma((n,)), dma((n,)),
                dma((doms,)), dma((doms,)), dma((doms,)), dma((doms,)), dma((2, doms)), dma((2, doms)),
            ],
            compiler_params=pltpu.CompilerParams(
                collective_id=0, has_side_effects=True, vmem_limit_bytes=32 * 1024 * 1024),
        )(*[pltpu.with_memory_space_constraint(x, pltpu.HBM) for x in operands])
        out_vec, out_rev, out_join = pl.pallas_call(
            place,
            out_shape=(shapes[0], jax.ShapeDtypeStruct((R, per), bf16), jax.ShapeDtypeStruct((R, per), bf16)),
            in_specs=[vmem, vmem],
            out_specs=(vmem, vmem, vmem),
            compiler_params=pltpu.CompilerParams(vmem_limit_bytes=8 * 1024 * 1024),
        )(found_vec, found_rows)
        return out_vec[None], out_rev.T[None], out_join.T[None]

    return jax.shard_map(
        per_device,
        mesh=mesh,
        in_specs=(
            P("dom", "pts", None),
            P("dom", "pts", None),
            P("dom", "pts", None),
            P("dom", "pts"),
        ),
        out_specs=(P("dom", "pts", None), P("dom", "pts", None), P("dom", "pts", None)),
        check_vma=False,
    )
```

```python
import functools

import jax
import jax.numpy as jnp
from jax import lax
from jax.experimental import pallas as pl
from jax.experimental.pallas import tpu as pltpu
from jax.sharding import PartitionSpec as P

R = 32
BIG = 1.0e9
NT = (((1,), (1,)), ((), ()))

START = (0, 1, 2, 4, 3)
SORT = (
    ((0,),),
    ((1,), (1, 2), (0,)),
    ((1,), (1, 2), (1,), (0,)),
    ((0, 4), (0,), (0, 2), (0,), (1,), (1, 4), (1,)),
    ((1, 3), (1,), (1, 2), (1,), (0,), (0, 4), (0,), (0, 3), (0,)),
)
MERGE = ((0, 3), (0, 2), (0,), (0, 2), (0, 4), (1,), (0,), (0, 4), (0,), (0, 3), (0,))
FINISH = ((0, 2),)


FIRST = 3
LATER = ((1, 2, 3, 4, 11, 5, 6, 7, 12, 14, 13, 15), (1, 2, 3, 4, 5, 6, 11, 7, 12, 13, 14, 15))
ORDER = (8, 9, 10, 1, 2, 3, 4, 11, 5, 6, 7, 12, 13, 14, 15)
WAIT = (8, 1, 9, 2, 3, 10, 4, 5, 11, 6, 7, 12, 13, 14, 15)


def dot(a, b):
    return jnp.dot(a, b, preferred_element_type=jnp.float32)


def dot_nt(a, b):
    return lax.dot_general(a, b, NT, preferred_element_type=jnp.float32)


def iota(shape, dim):
    return lax.broadcasted_iota(jnp.int32, shape, dim)


def onehot(cond):
    return jnp.where(cond, 1.0, 0.0).astype(jnp.bfloat16)


def pairs_along(bit):
    return [(i, i | 1 << bit) for i in range(4) if not i >> bit & 1]


def run_steps(items, steps, falling=False):
    items = list(items)
    place = iota(items[0].shape, 0)
    for step in steps:
        for i, j in pairs_along(step[0]):
            a, b = items[i], items[j]
            if len(step) == 1:
                low, high = jnp.minimum(a, b), jnp.maximum(a, b)
                items[i], items[j] = (high, low) if falling else (low, high)
            else:
                far = 1 << step[1] - 2
                first = (place & far) == 0
                items[i] = jnp.where(first, a, pltpu.roll(b, far, 0))
                items[j] = jnp.where(first, pltpu.roll(a, 8 - far, 0), b)
    return items


def flip(items, bits):
    place = iota(items[0].shape, 0)
    rows = [b - 2 for b in bits if b > 1]
    out = []
    for i, x in enumerate(items):
        odd = sum(i >> b & 1 for b in bits if b < 2) & 1
        if rows:
            total = sum((place >> s) & 1 for s in rows)
            sign = jnp.where((total & 1) == odd, 1.0, -1.0)
            x = x * sign
        elif odd:
            x = -x
        out.append(x)
    return out


def sort_falling(items):
    where = list(START)
    negated = None
    for phase, steps in enumerate(SORT):
        bit = phase + 1
        bits = []
        if negated is not None:
            bits.append(where.index(negated))
        negated = bit if bit < 5 else None
        if negated is not None:
            bits.append(where.index(negated))
        items = flip(items, bits)
        items = run_steps(items, steps, falling=bit == 5)
        for step in steps:
            if len(step) == 2:
                v, s = step
                where[v], where[s] = where[s], where[v]
    return items


def merge_low(rising, falling):
    return run_steps([jnp.minimum(a, b) for a, b in zip(rising, falling)], MERGE)


def kernel(n, doms, cap, order, *refs):
    refs = list(refs)
    vec, shards_hbm, locs_hbm, part_hbm = refs[:4]
    refs = refs[4:]
    wide = shards_hbm.shape[0] > 1
    slot_shard_hbm = refs.pop(0) if wide else None
    out_vec, out_rows = refs[:2]
    (own_ref, shards_t, locs, part, slot_shard, sbuf, sinfo, rvec, rinfo, dvec, dpart, posn, ltile, lshard, selfid,
     onorm, best, picks, srows, drows,
     in_sem, vs_sem, vr_sem, is_sem, ir_sem, ds_sem, dr_sem, ps_sem, pr_sem, rs_sem, rr_sem, seen, across, rest) = refs[2:]
    per, depth = vec.shape
    list_len = locs.shape[0]
    groups = cap // 8
    lanes = groups * list_len
    me = lax.axis_index("pts")
    dom = lax.axis_index("dom")
    bar = pltpu.get_barrier_semaphore()
    bits = [1 << b for b in range(n.bit_length() - 1)]

    def partner(o):
        swap = (o // (n // 2)) * (1 - me // (n // 2))
        out = me
        for b in bits:
            odd = lax.rem(o // b, 2)
            if b == n // 4:
                odd = odd + swap - 2 * odd * swap
            out = out + odd * (b - 2 * b * lax.rem(me // b, 2))
        return out

    def greet_pts(o, carry):
        pl.semaphore_signal(bar, inc=1, device_id={"pts": lax.rem(me + o, n)}, device_id_type=pl.DeviceIdType.MESH)
        return carry

    def greet_dom(o, carry):
        pl.semaphore_signal(bar, inc=1, device_id={"dom": lax.rem(dom + o, doms)}, device_id_type=pl.DeviceIdType.MESH)
        return carry

    half, quarter = n // 2, n // 4
    side = me // half

    def tell(sem, **device):
        pl.semaphore_signal(sem, inc=1, device_id=device, device_id_type=pl.DeviceIdType.MESH)

    if order is None:
        lax.fori_loop(1, n, greet_pts, 0)
        lax.fori_loop(1, doms, greet_dom, 0)
    else:
        @pl.when(side == 0)
        def _():
            for o in range(n - 1, 0, -1):
                tell(bar, pts=partner(o))
            lax.fori_loop(1, doms, greet_dom, 0)

    fetch_shards = pltpu.make_async_copy(shards_hbm, shards_t, in_sem.at[0])
    fetch_locs = pltpu.make_async_copy(locs_hbm, locs, in_sem.at[1])
    fetch_part = pltpu.make_async_copy(part_hbm, part, in_sem.at[2])
    fetch_vec = pltpu.make_async_copy(vec, own_ref, in_sem.at[3])
    fetch_shards.start()
    fetch_vec.start()
    fetch_locs.start()
    if wide:
        fetch_slots = pltpu.make_async_copy(slot_shard_hbm, slot_shard, in_sem.at[4])
        fetch_slots.start()
    fetch_part.start()
    if order is not None:
        @pl.when(side == 1)
        def _():
            pl.semaphore_wait(bar, half)
            for o in range(half, n):
                tell(seen.at[lax.rem(me // quarter, 2)], pts=partner(o))


    upper = onehot(iota((per, per), 0) < iota((per, per), 1))
    tile = onehot(lax.rem(iota((list_len, lanes), 1), list_len) == iota((list_len, lanes), 0))
    targets = partner(iota((n, per), 0))
    lane_group = iota((8, lanes), 1) // list_len
    slot_row = iota((cap, per), 0).astype(jnp.float32)

    fetch_shards.wait()
    member = shards_t[0:1, :] == targets
    for w in range(1, shards_t.shape[0]):
        member = member | (shards_t[w : w + 1, :] == targets)
    rank = dot(onehot(member), upper)
    posn[...] = jnp.where(member, rank, -1.0)

    def spread(ref):
        return lax.dot_general(ref[...].astype(jnp.float32).astype(jnp.bfloat16), tile, (((0,), (0,)), ((), ())),
                               preferred_element_type=jnp.float32)

    def tile_lists():
        fetch_locs.wait()
        ltile[...] = (spread(locs) + 1.0).astype(jnp.bfloat16)
        if wide:
            fetch_slots.wait()
            lshard[...] = spread(slot_shard)

    fetch_vec.wait()

    def fold(full):
        flat = jnp.zeros((8, lanes), jnp.float32)
        for g in range(groups):
            flat = jnp.where(lane_group == g, full[8 * g : 8 * g + 8], flat)
        return flat.astype(jnp.bfloat16)

    def picks_of(offsets):
        return [onehot(posn[pl.ds(o, 1), :] == slot_row) for o in offsets]

    def pack_vec(slots, offsets):
        packed = dot(jnp.concatenate(picks_of(offsets), axis=0), own_ref[...]).astype(jnp.bfloat16)
        for t, i in enumerate(slots):
            sbuf[i] = packed[t * cap : t * cap + cap]

    def pack_info(slots, offsets):
        chosen = picks_of(offsets)
        if not wide:
            full = dot(jnp.concatenate(chosen, axis=0), ltile[...])
        for t, (i, o) in enumerate(zip(slots, offsets)):
            if wide:
                c = partner(o)
                entry = jnp.where(lshard[...] == c.astype(jnp.float32), ltile[...].astype(jnp.float32), 0.0)
                sinfo[i] = fold(dot(chosen[t], entry.astype(jnp.bfloat16)))
            else:
                sinfo[i] = fold(full[t * cap : t * cap + cap])

    def vec_copy(i, c):
        return pltpu.make_async_remote_copy(
            src_ref=sbuf.at[i], dst_ref=rvec.at[i], send_sem=vs_sem.at[i], recv_sem=vr_sem.at[i],
            device_id={"pts": c}, device_id_type=pl.DeviceIdType.MESH)

    def info_copy(i, c):
        return pltpu.make_async_remote_copy(
            src_ref=sinfo.at[i], dst_ref=rinfo.at[i], send_sem=is_sem.at[i], recv_sem=ir_sem.at[i],
            device_id={"pts": c}, device_id_type=pl.DeviceIdType.MESH)

    def dom_copy(c, slot_r, src, dst, send, recv):
        return pltpu.make_async_remote_copy(
            src_ref=src, dst_ref=dst.at[slot_r], send_sem=send.at[c], recv_sem=recv.at[slot_r],
            device_id={"dom": c}, device_id_type=pl.DeviceIdType.MESH)

    def send(copy, i, o):
        copy(i, partner(o)).start()

    def send_dom(o, carry):
        c = lax.rem(dom + o, doms)
        dom_copy(c, dom, part, dpart, ps_sem, pr_sem).start()
        dom_copy(c, dom, own_ref, dvec, ds_sem, dr_sem).start()
        return carry

    def arrived():
        fetch_part.wait()
        pl.semaphore_wait(bar, n - 1 + doms - 1)
        lax.fori_loop(1, doms, send_dom, 0)

    if order is not None:
        whole = [(1 + WAIT.index(o), o) for o in order] + [(0, 0)]
        first, others = whole[:FIRST], whole[FIRST:]

        def pack_some(pack, some):
            pack([i for i, _ in some], [o for _, o in some])

        pack_some(pack_vec, first)

        @pl.when(side == 0)
        def _():
            pl.semaphore_wait(bar, half - 1 + doms - 1)
            pl.semaphore_wait(seen.at[1 - lax.rem(me // quarter, 2)], quarter)

        for i, o in first:
            send(vec_copy, i, o)
        tile_lists()
        pack_some(pack_info, whole)
        for i, o in first:
            send(info_copy, i, o)
        for at in range(0, len(others), 4):
            pack_some(pack_vec, others[at : at + 4])
        fetch_part.wait()

        @pl.when(side == 0)
        def _():
            pl.semaphore_wait(seen.at[lax.rem(me // quarter, 2)], quarter)
            for o in range(1, doms):
                tell(across, dom=lax.rem(dom + o, doms))

        @pl.when(side == 1)
        def _():
            pl.semaphore_wait(rest, 1)

        lax.fori_loop(1, doms, send_dom, 0)
        for number, later in enumerate(LATER):
            @pl.when(side == number)
            def _():
                for o in later:
                    send(info_copy, 1 + WAIT.index(o), o)
                    send(vec_copy, 1 + WAIT.index(o), o)


        @pl.when(side == 0)
        def _():
            pl.semaphore_wait(across, doms - 1)
            tell(rest, pts=me + half)

    else:
        tile_lists()

        def pack_loop(b, carry):
            some = [b * 4 + t for t in range(4)]
            pack_vec(some, some)
            pack_info(some, some)
            return carry

        def send_loop(o, carry):
            send(info_copy, o, o)
            send(vec_copy, o, o)
            return carry

        lax.fori_loop(0, n // 4, pack_loop, 0)
        arrived()
        lax.fori_loop(1, n, send_loop, 0)

    own = own_ref[...]
    square = jnp.square(own.astype(jnp.float32))
    high = square.astype(jnp.bfloat16)
    low = (square - high.astype(jnp.float32)).astype(jnp.bfloat16)
    ones = jnp.ones((8, depth), jnp.bfloat16)
    onorm[...] = dot_nt(ones, high) + dot_nt(ones, low)
    id_tile = (iota((per, 128), 0) + 1).astype(jnp.float32).astype(jnp.bfloat16)
    selfid[...] = dot(onehot(posn[0:1, :] == slot_row), id_tile)
    dvec[dom] = own
    dpart[dom] = part[...]
    width = shards_t.shape[0]
    for which in range(2):
        for v in range(4):
            best[which, v] = jnp.full((8, per), BIG, jnp.float32)

    def join(vectors, info, same):
        cand = vectors[...]
        wide_cand = cand.astype(jnp.float32)
        norm = jnp.sum(wide_cand * wide_cand, axis=1, keepdims=True)
        value = (onorm[0:1, :] + norm - 2.0 * dot_nt(cand, own_ref[...])) * (1.0 / depth)
        entry = info[...].astype(jnp.float32)
        point = (iota((8, per), 1) + 1).astype(jnp.float32)
        reverse, joined = [], []
        for g in range(groups):
            at = g * list_len
            listed = entry[:, at : at + 1] == point
            for k in range(1, list_len):
                listed = listed | (entry[:, at + k : at + k + 1] == point)
            allowed = entry[:, at : at + 1] > 0.0
            for w in range(1, width):
                allowed = allowed | (entry[:, at + w : at + w + 1] > 0.0)
            if same:
                allowed = allowed & (selfid[8 * g : 8 * g + 8, 0:1] != point)
            block = jnp.where(allowed, value[8 * g : 8 * g + 8], BIG)
            joined.append(block)
            reverse.append(jnp.where(listed, block, BIG))
        return reverse, joined

    def add(which, block):
        items = merge_low([best[which, v] for v in range(4)], sort_falling(block))
        for v in range(4):
            best[which, v] = items[v]

    def add_both(vectors, info, same):
        blocks = join(vectors, info, same)
        for which in range(2):
            add(which, blocks[which])

    add_both(sbuf.at[0], sinfo.at[0], True)
    other = lax.rem(me + 1, n)

    def take(i, carry):
        info_copy(i, other).wait_recv()
        vec_copy(i, other).wait_recv()
        add_both(rvec.at[i], rinfo.at[i], False)
        return carry

    def take_dom(o, carry):
        s = lax.rem(dom + doms - o, doms)
        dom_copy(s, s, part, dpart, ps_sem, pr_sem).wait_recv()
        dom_copy(s, s, own_ref, dvec, ds_sem, dr_sem).wait_recv()
        return carry

    lax.fori_loop(1, n // 2, take, 0)
    lax.fori_loop(1, doms, take_dom, 0)
    base = jnp.zeros((8, 1), jnp.float32)
    total = jnp.zeros((per, depth), jnp.float32)
    for d in range(doms):
        here = jnp.broadcast_to(dpart[d], (8, per)) == dom
        flag = jnp.where(here, 1.0, 0.0)
        place = jnp.where(here, dot(flag.astype(jnp.bfloat16), upper) + base, -1.0)
        base = base + jnp.sum(flag, axis=1, keepdims=True)
        pick = onehot(place[0:1, :] == iota((per, per), 0).astype(jnp.float32))
        picks[d] = pick
        total = total + dot(pick, dvec[d])
    out_vec[...] = total.astype(jnp.bfloat16)
    lax.fori_loop(n // 2, n - 1, take, 0)
    info_copy(n - 1, other).wait_recv()
    vec_copy(n - 1, other).wait_recv()
    blocks = join(rvec.at[n - 1], rinfo.at[n - 1], False)

    def rows_copy(c, slot_r, which):
        return pltpu.make_async_remote_copy(
            src_ref=srows.at[which], dst_ref=drows.at[slot_r, which], send_sem=rs_sem.at[which, c],
            recv_sem=rr_sem.at[which, slot_r], device_id={"dom": c}, device_id_type=pl.DeviceIdType.MESH)

    for which in range(2):
        items = merge_low([best[which, v] for v in range(4)], sort_falling(blocks[which]))
        items = run_steps(items, FINISH)
        items = [items[v >> 1 | (v & 1) << 1] for v in range(4)]
        rows = jnp.concatenate([jnp.where(x < 0.5 * BIG, x, 0.0) for x in items], axis=0)
        srows[which] = rows.astype(jnp.bfloat16)

        def send_rows(o, carry):
            rows_copy(lax.rem(dom + o, doms), dom, which).start()
            return carry

        lax.fori_loop(1, doms, send_rows, 0)

    def drain_pts(i, carry):
        info_copy(i, other).wait_send()
        vec_copy(i, other).wait_send()
        return carry

    def drain_dom(o, carry):
        c = lax.rem(dom + o, doms)
        dom_copy(c, dom, part, dpart, ps_sem, pr_sem).wait_send()
        dom_copy(c, dom, own_ref, dvec, ds_sem, dr_sem).wait_send()
        return carry

    lax.fori_loop(1, n, drain_pts, 0)
    lax.fori_loop(1, doms, drain_dom, 0)
    moved = dot_nt(jnp.concatenate([srows[0], srows[1]], axis=0), picks[dom])
    for o in range(1, doms):
        s = lax.rem(dom + doms - o, doms)
        rows_copy(s, s, 0).wait_recv()
        rows_copy(s, s, 1).wait_recv()
        moved = moved + dot_nt(jnp.concatenate([drows[s, 0], drows[s, 1]], axis=0), picks[s])
    out_rows[...] = moved.astype(jnp.bfloat16)
    for o in range(1, doms):
        c = lax.rem(dom + o, doms)
        rows_copy(c, dom, 0).wait_send()
        rows_copy(c, dom, 1).wait_send()


def place(found_vec, found_rows, out_vec, out_rev, out_join):
    out_vec[...] = found_vec[...]
    out_rev[...] = found_rows[:R]
    out_join[...] = found_rows[R:]


def solution(mesh):
    n, doms = mesh.shape["pts"], mesh.shape["dom"]
    order = ORDER if n == 16 else None

    def per_device(vectors, neighbor_shards, neighbor_locals, partition):
        per, depth = vectors.shape[1:]
        width = neighbor_shards.shape[2]
        list_len = neighbor_locals.shape[2]
        cap = per // 8
        lanes = (cap // 8) * list_len
        assert cap == R
        operands = [vectors[0], neighbor_shards[0].T, neighbor_locals[0].T, partition]
        if width > 1:
            operands.append(neighbor_shards[0].T[jnp.arange(list_len) % width])
        bf16, f32, i32 = jnp.bfloat16, jnp.float32, jnp.int32
        dma = pltpu.SemaphoreType.DMA
        vmem = pl.BlockSpec(memory_space=pltpu.VMEM)
        anywhere = pl.BlockSpec(memory_space=pltpu.HBM)
        shapes = (jax.ShapeDtypeStruct((per, depth), bf16), jax.ShapeDtypeStruct((2 * R, per), bf16))
        found_vec, found_rows = pl.pallas_call(
            functools.partial(kernel, n, doms, cap, order),
            out_shape=shapes,
            in_specs=[anywhere] * len(operands),
            out_specs=(vmem, vmem),
            scratch_shapes=[
                pltpu.VMEM((per, depth), bf16),
                pltpu.VMEM((width, per), i32),
                pltpu.VMEM((list_len, per), i32),
                pltpu.VMEM((1, per), i32),
                pltpu.VMEM((list_len, per), i32),
                pltpu.VMEM((n, cap, depth), bf16),
                pltpu.VMEM((n, 8, lanes), bf16),
                pltpu.VMEM((n, cap, depth), bf16),
                pltpu.VMEM((n, 8, lanes), bf16),
                pltpu.VMEM((doms, per, depth), bf16),
                pltpu.VMEM((doms, 1, per), i32),
                pltpu.VMEM((n, per), f32),
                pltpu.VMEM((per, lanes), bf16),
                pltpu.VMEM((per, lanes), f32),
                pltpu.VMEM((cap, 128), f32),
                pltpu.VMEM((8, per), f32),
                pltpu.VMEM((2, 4, 8, per), f32),
                pltpu.VMEM((doms, per, per), bf16),
                pltpu.VMEM((2, R, per), bf16),
                pltpu.VMEM((doms, 2, R, per), bf16),
                dma((5,)),
                dma((n,)), dma((n,)), dma((n,)), dma((n,)),
                dma((doms,)), dma((doms,)), dma((doms,)), dma((doms,)), dma((2, doms)), dma((2, doms)),
                pltpu.SemaphoreType.REGULAR((2,)), pltpu.SemaphoreType.REGULAR, pltpu.SemaphoreType.REGULAR,
            ],
            compiler_params=pltpu.CompilerParams(
                collective_id=0, has_side_effects=True, vmem_limit_bytes=32 * 1024 * 1024),
        )(*[pltpu.with_memory_space_constraint(x, pltpu.HBM) for x in operands])
        out_vec, out_rev, out_join = pl.pallas_call(
            place,
            out_shape=(shapes[0], jax.ShapeDtypeStruct((R, per), bf16), jax.ShapeDtypeStruct((R, per), bf16)),
            in_specs=[vmem, vmem],
            out_specs=(vmem, vmem, vmem),
            compiler_params=pltpu.CompilerParams(vmem_limit_bytes=8 * 1024 * 1024),
        )(found_vec, found_rows)
        return out_vec[None], out_rev.T[None], out_join.T[None]

    return jax.shard_map(
        per_device,
        mesh=mesh,
        in_specs=(
            P("dom", "pts", None),
            P("dom", "pts", None),
            P("dom", "pts", None),
            P("dom", "pts"),
        ),
        out_specs=(P("dom", "pts", None), P("dom", "pts", None), P("dom", "pts", None)),
        check_vma=False,
    )
```

```python
import functools

import jax
import jax.numpy as jnp
from jax import lax
from jax.experimental import pallas as pl
from jax.experimental.pallas import tpu as pltpu
from jax.sharding import PartitionSpec as P

R = 32
BIG = 1.0e9
NT = (((1,), (1,)), ((), ()))

START = (0, 1, 2, 4, 3)
SORT = (
    ((0,),),
    ((1,), (1, 2), (0,)),
    ((1,), (1, 2), (1,), (0,)),
    ((0, 4), (0,), (0, 2), (0,), (1,), (1, 4), (1,)),
    ((1, 3), (1,), (1, 2), (1,), (0,), (0, 4), (0,), (0, 3), (0,)),
)
MERGE = ((0, 3), (0, 2), (0,), (0, 2), (0, 4), (1,), (0,), (0, 4), (0,), (0, 3), (0,))
FINISH = ((0, 2),)


FIRST = 3
LATER = ((1, 2, 3, 4, 11, 5, 6, 7, 12, 14, 13, 15), (1, 2, 3, 4, 5, 6, 11, 7, 12, 13, 14, 15))
ORDER = (8, 9, 10, 1, 2, 3, 4, 11, 5, 6, 7, 12, 13, 14, 15)
WAIT = (8, 1, 9, 2, 3, 10, 4, 5, 11, 6, 7, 12, 13, 14, 15)


def dot(a, b):
    return jnp.dot(a, b, preferred_element_type=jnp.float32)


def dot_nt(a, b):
    return lax.dot_general(a, b, NT, preferred_element_type=jnp.float32)


def iota(shape, dim):
    return lax.broadcasted_iota(jnp.int32, shape, dim)


def onehot(cond):
    return jnp.where(cond, 1.0, 0.0).astype(jnp.bfloat16)


def pairs_along(bit):
    return [(i, i | 1 << bit) for i in range(4) if not i >> bit & 1]


def run_steps(items, steps, falling=False):
    items = list(items)
    place = iota(items[0].shape, 0)
    for step in steps:
        for i, j in pairs_along(step[0]):
            a, b = items[i], items[j]
            if len(step) == 1:
                low, high = jnp.minimum(a, b), jnp.maximum(a, b)
                items[i], items[j] = (high, low) if falling else (low, high)
            else:
                far = 1 << step[1] - 2
                first = (place & far) == 0
                items[i] = jnp.where(first, a, pltpu.roll(b, far, 0))
                items[j] = jnp.where(first, pltpu.roll(a, 8 - far, 0), b)
    return items


def flip(items, bits):
    place = iota(items[0].shape, 0)
    rows = [b - 2 for b in bits if b > 1]
    out = []
    for i, x in enumerate(items):
        odd = sum(i >> b & 1 for b in bits if b < 2) & 1
        if rows:
            total = sum((place >> s) & 1 for s in rows)
            sign = jnp.where((total & 1) == odd, 1.0, -1.0)
            x = x * sign
        elif odd:
            x = -x
        out.append(x)
    return out


def sort_falling(items):
    where = list(START)
    negated = None
    for phase, steps in enumerate(SORT):
        bit = phase + 1
        bits = []
        if negated is not None:
            bits.append(where.index(negated))
        negated = bit if bit < 5 else None
        if negated is not None:
            bits.append(where.index(negated))
        items = flip(items, bits)
        items = run_steps(items, steps, falling=bit == 5)
        for step in steps:
            if len(step) == 2:
                v, s = step
                where[v], where[s] = where[s], where[v]
    return items


def merge_low(rising, falling):
    return run_steps([jnp.minimum(a, b) for a, b in zip(rising, falling)], MERGE)


def kernel(n, doms, cap, order, *refs):
    refs = list(refs)
    vec, shards_hbm, locs_hbm, part_hbm = refs[:4]
    refs = refs[4:]
    wide = shards_hbm.shape[0] > 1
    slot_shard_hbm = refs.pop(0) if wide else None
    out_vec, out_rows = refs[:2]
    (own_ref, shards_t, locs, part, slot_shard, sbuf, sinfo, rvec, rinfo, dvec, dpart, posn, ltile, lshard, selfid,
     onorm, best, picks, srows, drows,
     in_sem, vs_sem, vr_sem, is_sem, ir_sem, ds_sem, dr_sem, ps_sem, pr_sem, rs_sem, rr_sem, seen, across, rest) = refs[2:]
    per, depth = vec.shape
    list_len = locs.shape[0]
    groups = cap // 8
    lanes = groups * list_len
    me = lax.axis_index("pts")
    dom = lax.axis_index("dom")
    bar = pltpu.get_barrier_semaphore()
    bits = [1 << b for b in range(n.bit_length() - 1)]

    def partner(o):
        swap = (o // (n // 2)) * (1 - me // (n // 2))
        out = me
        for b in bits:
            odd = lax.rem(o // b, 2)
            if b == n // 4:
                odd = odd + swap - 2 * odd * swap
            out = out + odd * (b - 2 * b * lax.rem(me // b, 2))
        return out

    def greet_pts(o, carry):
        pl.semaphore_signal(bar, inc=1, device_id={"pts": lax.rem(me + o, n)}, device_id_type=pl.DeviceIdType.MESH)
        return carry

    def greet_dom(o, carry):
        pl.semaphore_signal(bar, inc=1, device_id={"dom": lax.rem(dom + o, doms)}, device_id_type=pl.DeviceIdType.MESH)
        return carry

    half, quarter = n // 2, n // 4
    side = me // half

    def tell(sem, **device):
        pl.semaphore_signal(sem, inc=1, device_id=device, device_id_type=pl.DeviceIdType.MESH)

    if order is None:
        lax.fori_loop(1, n, greet_pts, 0)
        lax.fori_loop(1, doms, greet_dom, 0)
    else:
        @pl.when(side == 0)
        def _():
            for o in range(n - 1, 0, -1):
                tell(bar, pts=partner(o))
            lax.fori_loop(1, doms, greet_dom, 0)

    fetch_shards = pltpu.make_async_copy(shards_hbm, shards_t, in_sem.at[0])
    fetch_locs = pltpu.make_async_copy(locs_hbm, locs, in_sem.at[1])
    fetch_part = pltpu.make_async_copy(part_hbm, part, in_sem.at[2])
    fetch_vec = pltpu.make_async_copy(vec, own_ref, in_sem.at[3])
    fetch_shards.start()
    fetch_vec.start()
    fetch_locs.start()
    if wide:
        fetch_slots = pltpu.make_async_copy(slot_shard_hbm, slot_shard, in_sem.at[4])
        fetch_slots.start()
    fetch_part.start()
    if order is not None:
        @pl.when(side == 1)
        def _():
            pl.semaphore_wait(bar, half)
            for o in range(half, n):
                tell(seen.at[lax.rem(me // quarter, 2)], pts=partner(o))


    upper = onehot(iota((per, per), 0) < iota((per, per), 1))
    tile = onehot(lax.rem(iota((list_len, lanes), 1), list_len) == iota((list_len, lanes), 0))
    targets = partner(iota((n, per), 0))
    lane_group = iota((8, lanes), 1) // list_len
    slot_row = iota((cap, per), 0).astype(jnp.float32)

    fetch_shards.wait()
    member = shards_t[0:1, :] == targets
    for w in range(1, shards_t.shape[0]):
        member = member | (shards_t[w : w + 1, :] == targets)
    rank = dot(onehot(member), upper)
    posn[...] = jnp.where(member, rank, -1.0)

    def spread(ref):
        return lax.dot_general(ref[...].astype(jnp.float32).astype(jnp.bfloat16), tile, (((0,), (0,)), ((), ())),
                               preferred_element_type=jnp.float32)

    def tile_lists():
        fetch_locs.wait()
        ltile[...] = (spread(locs) + 1.0).astype(jnp.bfloat16)
        if wide:
            fetch_slots.wait()
            lshard[...] = spread(slot_shard)

    fetch_vec.wait()

    def fold(full):
        flat = jnp.zeros((8, lanes), jnp.float32)
        for g in range(groups):
            flat = jnp.where(lane_group == g, full[8 * g : 8 * g + 8], flat)
        return flat.astype(jnp.bfloat16)

    def picks_of(offsets):
        return [onehot(posn[pl.ds(o, 1), :] == slot_row) for o in offsets]

    def pack_vec(slots, offsets):
        packed = dot(jnp.concatenate(picks_of(offsets), axis=0), own_ref[...]).astype(jnp.bfloat16)
        for t, i in enumerate(slots):
            sbuf[i] = packed[t * cap : t * cap + cap]

    def pack_info(slots, offsets):
        chosen = picks_of(offsets)
        if not wide:
            full = dot(jnp.concatenate(chosen, axis=0), ltile[...])
        for t, (i, o) in enumerate(zip(slots, offsets)):
            if wide:
                c = partner(o)
                entry = jnp.where(lshard[...] == c.astype(jnp.float32), ltile[...].astype(jnp.float32), 0.0)
                sinfo[i] = fold(dot(chosen[t], entry.astype(jnp.bfloat16)))
            else:
                sinfo[i] = fold(full[t * cap : t * cap + cap])

    def vec_copy(i, c):
        return pltpu.make_async_remote_copy(
            src_ref=sbuf.at[i], dst_ref=rvec.at[i], send_sem=vs_sem.at[i], recv_sem=vr_sem.at[i],
            device_id={"pts": c}, device_id_type=pl.DeviceIdType.MESH)

    def info_copy(i, c):
        return pltpu.make_async_remote_copy(
            src_ref=sinfo.at[i], dst_ref=rinfo.at[i], send_sem=is_sem.at[i], recv_sem=ir_sem.at[i],
            device_id={"pts": c}, device_id_type=pl.DeviceIdType.MESH)

    def dom_copy(c, slot_r, src, dst, send, recv):
        return pltpu.make_async_remote_copy(
            src_ref=src, dst_ref=dst.at[slot_r], send_sem=send.at[c], recv_sem=recv.at[slot_r],
            device_id={"dom": c}, device_id_type=pl.DeviceIdType.MESH)

    def send(copy, i, o):
        copy(i, partner(o)).start()

    def send_dom(o, carry):
        c = lax.rem(dom + o, doms)
        dom_copy(c, dom, part, dpart, ps_sem, pr_sem).start()
        dom_copy(c, dom, own_ref, dvec, ds_sem, dr_sem).start()
        return carry

    def arrived():
        fetch_part.wait()
        pl.semaphore_wait(bar, n - 1 + doms - 1)
        lax.fori_loop(1, doms, send_dom, 0)

    if order is not None:
        whole = [(1 + WAIT.index(o), o) for o in order] + [(0, 0)]
        first, others = whole[:FIRST], whole[FIRST:]

        def pack_some(pack, some):
            pack([i for i, _ in some], [o for _, o in some])

        pack_some(pack_vec, first)

        @pl.when(side == 0)
        def _():
            pl.semaphore_wait(bar, half - 1 + doms - 1)
            pl.semaphore_wait(seen.at[1 - lax.rem(me // quarter, 2)], quarter)

        for i, o in first:
            send(vec_copy, i, o)
        tile_lists()
        pack_some(pack_info, whole)
        for i, o in first:
            send(info_copy, i, o)
        for at in range(0, len(others), 4):
            pack_some(pack_vec, others[at : at + 4])
        fetch_part.wait()

        @pl.when(side == 0)
        def _():
            pl.semaphore_wait(seen.at[lax.rem(me // quarter, 2)], quarter)
            for o in range(1, doms):
                tell(across, dom=lax.rem(dom + o, doms))

        @pl.when(side == 1)
        def _():
            pl.semaphore_wait(rest, 1)

        lax.fori_loop(1, doms, send_dom, 0)
        for number, later in enumerate(LATER):
            @pl.when(side == number)
            def _():
                for o in later:
                    send(info_copy, 1 + WAIT.index(o), o)
                    send(vec_copy, 1 + WAIT.index(o), o)


        @pl.when(side == 0)
        def _():
            pl.semaphore_wait(across, doms - 1)
            tell(rest, pts=me + half)

    else:
        tile_lists()

        def pack_loop(b, carry):
            some = [b * 4 + t for t in range(4)]
            pack_vec(some, some)
            pack_info(some, some)
            return carry

        def send_loop(o, carry):
            send(info_copy, o, o)
            send(vec_copy, o, o)
            return carry

        lax.fori_loop(0, n // 4, pack_loop, 0)
        arrived()
        lax.fori_loop(1, n, send_loop, 0)

    own = own_ref[...]
    square = jnp.square(own.astype(jnp.float32))
    high = square.astype(jnp.bfloat16)
    low = (square - high.astype(jnp.float32)).astype(jnp.bfloat16)
    ones = jnp.ones((8, depth), jnp.bfloat16)
    onorm[...] = dot_nt(ones, high) + dot_nt(ones, low)
    id_tile = (iota((per, 128), 0) + 1).astype(jnp.float32).astype(jnp.bfloat16)
    selfid[...] = dot(onehot(posn[0:1, :] == slot_row), id_tile)
    dvec[dom] = own
    dpart[dom] = part[...]
    width = shards_t.shape[0]
    for which in range(2):
        for v in range(4):
            best[which, v] = jnp.full((8, per), BIG, jnp.float32)

    def join(vectors, info, same, arrive=None):
        entry = info[...].astype(jnp.float32)
        point = (iota((8, per), 1) + 1).astype(jnp.float32)
        masks = []
        for g in range(groups):
            at = g * list_len
            listed = entry[:, at : at + 1] == point
            for k in range(1, list_len):
                listed = listed | (entry[:, at + k : at + k + 1] == point)
            allowed = entry[:, at : at + 1] > 0.0
            for w in range(1, width):
                allowed = allowed | (entry[:, at + w : at + w + 1] > 0.0)
            if same:
                allowed = allowed & (selfid[8 * g : 8 * g + 8, 0:1] != point)
            masks.append((listed, allowed))
        if arrive is not None:
            arrive.wait_recv()
        cand = vectors[...]
        wide_cand = cand.astype(jnp.float32)
        norm = jnp.sum(wide_cand * wide_cand, axis=1, keepdims=True)
        value = (onorm[0:1, :] + norm - 2.0 * dot_nt(cand, own_ref[...])) * (1.0 / depth)
        reverse, joined = [], []
        for g, (listed, allowed) in enumerate(masks):
            block = jnp.where(allowed, value[8 * g : 8 * g + 8], BIG)
            joined.append(block)
            reverse.append(jnp.where(listed, block, BIG))
        return reverse, joined

    def add(which, block):
        items = merge_low([best[which, v] for v in range(4)], sort_falling(block))
        for v in range(4):
            best[which, v] = items[v]

    def add_both(vectors, info, same):
        blocks = join(vectors, info, same)
        for which in range(2):
            add(which, blocks[which])

    add_both(sbuf.at[0], sinfo.at[0], True)
    other = lax.rem(me + 1, n)

    def take(i, carry):
        info_copy(i, other).wait_recv()
        vec_copy(i, other).wait_recv()
        add_both(rvec.at[i], rinfo.at[i], False)
        return carry

    def take_dom(o, carry):
        s = lax.rem(dom + doms - o, doms)
        dom_copy(s, s, part, dpart, ps_sem, pr_sem).wait_recv()
        dom_copy(s, s, own_ref, dvec, ds_sem, dr_sem).wait_recv()
        return carry

    lax.fori_loop(1, n // 2, take, 0)
    lax.fori_loop(1, doms, take_dom, 0)
    base = jnp.zeros((8, 1), jnp.float32)
    total = jnp.zeros((per, depth), jnp.float32)
    for d in range(doms):
        here = jnp.broadcast_to(dpart[d], (8, per)) == dom
        flag = jnp.where(here, 1.0, 0.0)
        place = jnp.where(here, dot(flag.astype(jnp.bfloat16), upper) + base, -1.0)
        base = base + jnp.sum(flag, axis=1, keepdims=True)
        pick = onehot(place[0:1, :] == iota((per, per), 0).astype(jnp.float32))
        picks[d] = pick
        total = total + dot(pick, dvec[d])
    out_vec[...] = total.astype(jnp.bfloat16)
    lax.fori_loop(n // 2, n - 1, take, 0)
    info_copy(n - 1, other).wait_recv()
    blocks = join(rvec.at[n - 1], rinfo.at[n - 1], False, vec_copy(n - 1, other))

    def rows_copy(c, slot_r, which):
        return pltpu.make_async_remote_copy(
            src_ref=srows.at[which], dst_ref=drows.at[slot_r, which], send_sem=rs_sem.at[which, c],
            recv_sem=rr_sem.at[which, slot_r], device_id={"dom": c}, device_id_type=pl.DeviceIdType.MESH)

    for which in range(2):
        items = merge_low([best[which, v] for v in range(4)], sort_falling(blocks[which]))
        items = run_steps(items, FINISH)
        items = [items[v >> 1 | (v & 1) << 1] for v in range(4)]
        rows = jnp.concatenate([jnp.where(x < 0.5 * BIG, x, 0.0) for x in items], axis=0)
        srows[which] = rows.astype(jnp.bfloat16)

        def send_rows(o, carry):
            rows_copy(lax.rem(dom + o, doms), dom, which).start()
            return carry

        lax.fori_loop(1, doms, send_rows, 0)

    def drain_pts(i, carry):
        info_copy(i, other).wait_send()
        vec_copy(i, other).wait_send()
        return carry

    def drain_dom(o, carry):
        c = lax.rem(dom + o, doms)
        dom_copy(c, dom, part, dpart, ps_sem, pr_sem).wait_send()
        dom_copy(c, dom, own_ref, dvec, ds_sem, dr_sem).wait_send()
        return carry

    lax.fori_loop(1, n, drain_pts, 0)
    lax.fori_loop(1, doms, drain_dom, 0)
    moved = dot_nt(jnp.concatenate([srows[0], srows[1]], axis=0), picks[dom])
    for o in range(1, doms):
        s = lax.rem(dom + doms - o, doms)
        rows_copy(s, s, 0).wait_recv()
        rows_copy(s, s, 1).wait_recv()
        moved = moved + dot_nt(jnp.concatenate([drows[s, 0], drows[s, 1]], axis=0), picks[s])
    out_rows[...] = moved.astype(jnp.bfloat16)
    for o in range(1, doms):
        c = lax.rem(dom + o, doms)
        rows_copy(c, dom, 0).wait_send()
        rows_copy(c, dom, 1).wait_send()


def place(found_vec, found_rows, out_vec, out_rev, out_join):
    out_vec[...] = found_vec[...]
    out_rev[...] = found_rows[:R]
    out_join[...] = found_rows[R:]


def solution(mesh):
    n, doms = mesh.shape["pts"], mesh.shape["dom"]
    order = ORDER if n == 16 else None

    def per_device(vectors, neighbor_shards, neighbor_locals, partition):
        per, depth = vectors.shape[1:]
        width = neighbor_shards.shape[2]
        list_len = neighbor_locals.shape[2]
        cap = per // 8
        lanes = (cap // 8) * list_len
        assert cap == R
        operands = [vectors[0], neighbor_shards[0].T, neighbor_locals[0].T, partition]
        if width > 1:
            operands.append(neighbor_shards[0].T[jnp.arange(list_len) % width])
        bf16, f32, i32 = jnp.bfloat16, jnp.float32, jnp.int32
        dma = pltpu.SemaphoreType.DMA
        vmem = pl.BlockSpec(memory_space=pltpu.VMEM)
        anywhere = pl.BlockSpec(memory_space=pltpu.HBM)
        shapes = (jax.ShapeDtypeStruct((per, depth), bf16), jax.ShapeDtypeStruct((2 * R, per), bf16))
        found_vec, found_rows = pl.pallas_call(
            functools.partial(kernel, n, doms, cap, order),
            out_shape=shapes,
            in_specs=[anywhere] * len(operands),
            out_specs=(vmem, vmem),
            scratch_shapes=[
                pltpu.VMEM((per, depth), bf16),
                pltpu.VMEM((width, per), i32),
                pltpu.VMEM((list_len, per), i32),
                pltpu.VMEM((1, per), i32),
                pltpu.VMEM((list_len, per), i32),
                pltpu.VMEM((n, cap, depth), bf16),
                pltpu.VMEM((n, 8, lanes), bf16),
                pltpu.VMEM((n, cap, depth), bf16),
                pltpu.VMEM((n, 8, lanes), bf16),
                pltpu.VMEM((doms, per, depth), bf16),
                pltpu.VMEM((doms, 1, per), i32),
                pltpu.VMEM((n, per), f32),
                pltpu.VMEM((per, lanes), bf16),
                pltpu.VMEM((per, lanes), f32),
                pltpu.VMEM((cap, 128), f32),
                pltpu.VMEM((8, per), f32),
                pltpu.VMEM((2, 4, 8, per), f32),
                pltpu.VMEM((doms, per, per), bf16),
                pltpu.VMEM((2, R, per), bf16),
                pltpu.VMEM((doms, 2, R, per), bf16),
                dma((5,)),
                dma((n,)), dma((n,)), dma((n,)), dma((n,)),
                dma((doms,)), dma((doms,)), dma((doms,)), dma((doms,)), dma((2, doms)), dma((2, doms)),
                pltpu.SemaphoreType.REGULAR((2,)), pltpu.SemaphoreType.REGULAR, pltpu.SemaphoreType.REGULAR,
            ],
            compiler_params=pltpu.CompilerParams(
                collective_id=0, has_side_effects=True, vmem_limit_bytes=32 * 1024 * 1024),
        )(*[pltpu.with_memory_space_constraint(x, pltpu.HBM) for x in operands])
        out_vec, out_rev, out_join = pl.pallas_call(
            place,
            out_shape=(shapes[0], jax.ShapeDtypeStruct((R, per), bf16), jax.ShapeDtypeStruct((R, per), bf16)),
            in_specs=[vmem, vmem],
            out_specs=(vmem, vmem, vmem),
            compiler_params=pltpu.CompilerParams(vmem_limit_bytes=8 * 1024 * 1024),
        )(found_vec, found_rows)
        return out_vec[None], out_rev.T[None], out_join.T[None]

    return jax.shard_map(
        per_device,
        mesh=mesh,
        in_specs=(
            P("dom", "pts", None),
            P("dom", "pts", None),
            P("dom", "pts", None),
            P("dom", "pts"),
        ),
        out_specs=(P("dom", "pts", None), P("dom", "pts", None), P("dom", "pts", None)),
        check_vma=False,
    )
```
